32 devices in a mesh: space: 8 (over y, x, core), chan: 4 (over z).
Axes of the slice: x: 2, y: 2, z: 4, core: 2. Of those that a mesh axis runs over, the one named last changes fastest.
Arguments:
- points: bfloat16 [256, 8, 16384], P('chan', 'space'), may hold values from -6 to 6
- point_cell: int32 [8, 16384], P('space'), may hold values from 0 to 4096, as said below
- conv_weight: bfloat16 [27, 256, 256], P(None, 'chan'), may hold values from -0.109375 to 0.109375
- conv_bias: bfloat16 [256], P('chan'), may hold values from -3 to 3
- neighbors: int32 [64, 27], P('space'), may hold values from -1 to 23, as said below
Outputs:
- voxel_out: bfloat16 [256, 32768], P('chan', 'space')
- point_out: bfloat16 [256, 8, 16384], P('chan', 'space')
The draws below stay inside these ranges and needn't reach their ends.
Inputs may be any that keep to these rules, and one draw needn't show every extreme that they name: `point_cell`: in each aligned block of 2048 slots from one sender the live slots (cell below 4096) come first; in every draw some owner receives 2048 live slots from every sender. `neighbors`: entry 13 is the block's own slot 8 + b; blocks of one owner lie on a 4 x (4) grid of a strip, strips of owners d and d+1 adjacent.
All inputs are finite; a program needn't handle non-finite values.
Results may differ from the reference program's by a relative error of at most 0.01.
Values may be sent and summed in bfloat16 or wider, within the bound.
A program may use at most 128 MiB of HBM per device.

```python
import jax
import jax.numpy as jnp
from jax import lax

C = 256
B_DEV = 8
PTS_DEV = 16384
N_SPACE = 8
N_CHAN = 4


def draw_point_cell(key, part):
    slot_cap = PTS_DEV // N_SPACE
    keys = jax.random.split(key, 5)
    levels = jnp.array([1, 1, 1, 2, 4], dtype=jnp.int32)
    owner_weight = levels[jax.random.randint(keys[0], (N_SPACE,), 0, 5)]
    busiest = jax.random.randint(keys[1], (), 0, N_SPACE)
    jitter = jax.random.randint(keys[2], (N_SPACE, N_SPACE), 0, slot_cap // 8 + 1)
    live_count = jnp.clip(slot_cap * owner_weight[:, None] // 4 - jitter, 0, slot_cap)
    owner_ids = jnp.arange(N_SPACE, dtype=jnp.int32)[:, None]
    live_count = jnp.where(owner_ids == busiest, slot_cap, live_count)
    block_id = jax.random.randint(keys[3], (N_SPACE, N_SPACE, slot_cap), 0, B_DEV)
    within = jax.random.randint(keys[4], (N_SPACE, N_SPACE, slot_cap), 0, 512)
    slot_ids = jnp.arange(slot_cap, dtype=jnp.int32)[None, None, :]
    cell_ids = jnp.where(slot_ids < live_count[:, :, None], block_id * 512 + within, B_DEV * 512)
    return cell_ids.reshape(N_SPACE, PTS_DEV).astype(jnp.int32)


def draw_neighbors(key, part):
    half_side = B_DEV // 2
    keys = jax.random.split(key, N_SPACE)
    orders = jax.vmap(lambda single: jax.random.permutation(single, 2 * B_DEV))(keys)
    places = orders[:, :B_DEV].astype(jnp.int32)
    coord_y = places // half_side
    coord_z = places % half_side
    owner_ids = jnp.arange(N_SPACE, dtype=jnp.int32)
    slot_ids = jnp.arange(B_DEV, dtype=jnp.int32)
    entries = []
    for shift_x in (-1, 0, 1):
        for shift_y in (-1, 0, 1):
            for shift_z in (-1, 0, 1):
                target_owner = owner_ids + shift_x
                owner_valid = (target_owner >= 0) & (target_owner < N_SPACE)
                clipped = jnp.clip(target_owner, 0, N_SPACE - 1)
                target_y = coord_y + shift_y
                target_z = coord_z + shift_z
                inside = (target_y >= 0) & (target_y < 4) & (target_z >= 0) & (target_z < half_side)
                target_place = target_y * half_side + target_z
                others = places[clipped]
                matches = others[:, None, :] == target_place[:, :, None]
                found = jnp.any(matches, axis=2)
                found_slot = jnp.sum(jnp.where(matches, slot_ids[None, None, :], 0), axis=2)
                entry = jnp.where(owner_valid[:, None] & inside & found, (shift_x + 1) * B_DEV + found_slot, -1)
                entries.append(entry)
    return jnp.stack(entries, 2).reshape(N_SPACE * B_DEV, 27).astype(jnp.int32)


def strengthened(values, key, source, target, shards_of, factor):
    owner, partner = [(jnp.arange(values.shape[dim]) // (values.shape[dim] // shards_of)).reshape([-1 if axis == dim else 1 for axis in range(values.ndim)]) for dim in (source, target)]
    chosen = jax.random.permutation(key, shards_of)[partner]
    strong = (owner == chosen) | (owner == (partner + shards_of // 2) % shards_of)
    return jnp.where(strong, factor * values, values)


def block_levels(rng, shape, cuts, least, top_value):
    level = 1.0
    for position, parts in cuts:
        steps = jax.random.uniform(jax.random.fold_in(jax.random.fold_in(rng, 6), position), (parts,), jnp.float32, least / len(cuts), top_value / len(cuts))
        level = level * jnp.repeat(jnp.exp(steps), shape[position] // parts).reshape((-1,) + (1,) * (len(shape) - 1 - position))
    return level


def bell_draw(own_key, extent, deviation, most, cuts=(), held_as=jnp.bfloat16):
    values = deviation * jax.random.normal(own_key, extent, jnp.float32)
    if cuts:
        values = values * block_levels(own_key, extent, cuts, -0.22, 0.18)
    return jnp.clip(values, -most, most).astype(held_as)


def gaussian_with(rng, shape, deviation, limit, cuts, heavy, kind=jnp.bfloat16):
    values = deviation * jax.random.normal(rng, shape, jnp.float32)
    if cuts:
        values = values * block_levels(rng, shape, cuts, -0.22, 0.18)
    return jnp.clip(strengthened(values, jax.random.fold_in(rng, 3), *heavy), -limit, limit).astype(kind)


def setup_inputs(seed: int = 0) -> dict:
    key_list = jax.random.split(jax.random.key(seed), 6)
    points = bell_draw(key_list[0], (C, N_SPACE, PTS_DEV), 1.0, 6.0, ((0, 4), (1, 8)))
    point_cell = draw_point_cell(jax.random.fold_in(key_list[5], 71), 0)
    conv_weight = gaussian_with(key_list[2], (27, C, C), (27 * C) ** -0.5, 0.109375, ((1, 4),), (1, 2, 4, 2.0))
    conv_bias = bell_draw(key_list[3], (C,), 0.5, 3.0, ((0, 4),))
    neighbors = draw_neighbors(jax.random.fold_in(key_list[5], 71), 0)
    return {"points": points, "point_cell": point_cell, "conv_weight": conv_weight, "conv_bias": conv_bias, "neighbors": neighbors}


def assemble(source, lookup):
    spare = source.shape[1] - 1
    picked = jnp.where(lookup < 0, spare, lookup).astype(jnp.int32)
    nearby = jnp.take(source, picked.reshape(-1), axis=1)
    width_here = source.shape[0]
    block_count = lookup.shape[0]
    nearby = nearby.reshape(width_here, block_count, 3, 3, 3, 8, 8, 8)
    nearby = jnp.transpose(nearby, (0, 1, 2, 5, 3, 6, 4, 7)).reshape(width_here, block_count, 24, 24, 24)
    return nearby[:, :, 7:17, 7:17, 7:17]


def columns(padded):
    width_here = padded.shape[0]
    block_count = padded.shape[1]
    pieces = []
    for shift_x in range(3):
        for shift_y in range(3):
            for shift_z in range(3):
                window = padded[:, :, shift_x:shift_x + 8, shift_y:shift_y + 8, shift_z:shift_z + 8]
                pieces.append(window.reshape(width_here, block_count * 512))
    return jnp.stack(pieces, 0).reshape(27 * width_here, block_count * 512)


def reference(points, point_cell, conv_weight, conv_bias, neighbors):
    slot_cap = PTS_DEV // N_SPACE
    width_all = points.shape[0]
    group_width = width_all // N_CHAN
    total_cells = B_DEV * 512

    def owner_pool(owner):
        arrived = lax.dynamic_slice_in_dim(points, owner * slot_cap, slot_cap, 2).reshape(width_all, N_SPACE * slot_cap)
        cell_ids = point_cell[owner]
        summed = jax.ops.segment_sum(arrived.astype(jnp.float32).T, cell_ids, num_segments=total_cells + 1)[:total_cells]
        tallies = jax.ops.segment_sum(jnp.ones(cell_ids.shape, jnp.float32), cell_ids, num_segments=total_cells + 1)[:total_cells]
        voxels = (summed / jnp.maximum(tallies, 1.0)[:, None]).astype(jnp.bfloat16)
        return voxels.T.reshape(width_all, B_DEV, 512), tallies

    voxels, tallies = lax.map(owner_pool, jnp.arange(N_SPACE, dtype=jnp.int32))
    border = jnp.zeros((1,) + voxels.shape[1:], voxels.dtype)
    widened = jnp.concatenate([border, voxels, border], 0)
    tables = neighbors.reshape(N_SPACE, B_DEV, 27)
    empty_block = jnp.zeros((width_all, 1, 512), voxels.dtype)
    bias_full = conv_bias.astype(jnp.float32)

    def owner_conv(owner):
        source = jnp.concatenate([widened[owner], widened[owner + 1], widened[owner + 2], empty_block], 1)
        padded = assemble(source, tables[owner])
        active = jnp.where(tallies[owner] > 0.0, 1.0, 0.0).astype(jnp.float32)
        total = jnp.zeros((width_all, total_cells), jnp.float32)
        for group in range(N_CHAN):
            low = group * group_width
            w_group = conv_weight[:, low:low + group_width, :].reshape(27 * group_width, width_all)
            stacked = columns(padded[low:low + group_width])
            partial_sum = jnp.dot(w_group.T, stacked, preferred_element_type=jnp.float32).astype(jnp.bfloat16)
            partial_sum = lax.optimization_barrier(partial_sum)
            total = total + partial_sum.astype(jnp.float32)
        result = (jnp.maximum(total + bias_full[:, None], 0.0) * active[None, :]).astype(jnp.bfloat16)
        extended = jnp.concatenate([result, jnp.zeros((width_all, 1), result.dtype)], 1)
        picked = jnp.take(extended, point_cell[owner], axis=1).reshape(width_all, N_SPACE, slot_cap)
        return result, picked

    results, picked = lax.map(owner_conv, jnp.arange(N_SPACE, dtype=jnp.int32))
    voxel_out = jnp.transpose(results, (1, 0, 2)).reshape(width_all, N_SPACE * total_cells)
    returned = jnp.transpose(picked, (1, 2, 0, 3)).reshape(width_all, N_SPACE, PTS_DEV)
    point_out = (points.astype(jnp.float32) + returned.astype(jnp.float32)).astype(jnp.bfloat16)
    return (voxel_out, point_out)
```

```python
import functools

import jax
import jax.numpy as jnp
from jax import lax
from jax.experimental import pallas as pl
from jax.experimental.pallas import tpu as pltpu
from jax.sharding import PartitionSpec as P

VMEM_LIMIT = 60 * 1024 * 1024
CELLS = 512
ROWS = 1008


def params():
    return pltpu.CompilerParams(vmem_limit_bytes=VMEM_LIMIT)


def split_kernel(x_ref, o_ref):
    o_ref[0] = x_ref[...]


def split_slots(points, owners, cap):
    width = points.shape[0]
    return pl.pallas_call(
        split_kernel,
        grid=(owners,),
        in_specs=[pl.BlockSpec((width, cap), lambda d: (0, d))],
        out_specs=pl.BlockSpec((1, width, cap), lambda d: (d, 0, 0)),
        out_shape=jax.ShapeDtypeStruct((owners, width, cap), jnp.bfloat16),
        compiler_params=params(),
    )(points)


def pool_kernel(groups, low_cells, x_ref, id_ref, count_ref, o_ref, acc_ref):
    turn = pl.program_id(0)
    width, rows = x_ref.shape[1], x_ref.shape[2]

    @pl.when(turn == 0)
    def _():
        acc_ref[...] = jnp.zeros_like(acc_ref)

    ids = id_ref[0]
    high = ids // low_cells
    low = ids % low_cells
    x = x_ref[0]
    zero = jnp.zeros_like(x)
    masked = jnp.concatenate(
        [jnp.where(jnp.broadcast_to(high, x.shape) == g, x, zero) for g in range(groups)], axis=0
    )
    spots = lax.broadcasted_iota(jnp.int32, (low_cells, rows), 0)
    onehot = jnp.where(spots == low, 1.0, 0.0).astype(jnp.bfloat16)
    acc_ref[...] += lax.dot_general(
        onehot, masked, (((1,), (1,)), ((), ())), preferred_element_type=jnp.float32
    )

    @pl.when(turn == pl.num_programs(0) - 1)
    def _():
        for g in range(groups):
            lanes = slice(g * width, (g + 1) * width)
            tally = jnp.maximum(count_ref[:, g : g + 1], 1.0)
            o_ref[:, lanes] = (acc_ref[:, lanes] / tally).astype(jnp.bfloat16)


def pool(arrived, ids, counts, groups):
    owners, width, cap = arrived.shape
    low_cells = counts.shape[0] // groups
    by_group = counts.reshape(groups, low_cells).T
    return pl.pallas_call(
        functools.partial(pool_kernel, groups, low_cells),
        grid=(owners,),
        in_specs=[
            pl.BlockSpec((1, width, cap), lambda s: (s, 0, 0)),
            pl.BlockSpec((1, 1, cap), lambda s: (s, 0, 0)),
            pl.BlockSpec((low_cells, groups), lambda s: (0, 0)),
        ],
        out_specs=pl.BlockSpec((low_cells, groups * width), lambda s: (0, 0)),
        out_shape=jax.ShapeDtypeStruct((low_cells, groups * width), jnp.bfloat16),
        scratch_shapes=[pltpu.VMEM((low_cells, groups * width), jnp.float32)],
        compiler_params=params(),
    )(arrived, ids.reshape(owners, 1, cap), by_group)


def margin_kernel(groups, share, nb_ref, left_ref, own_ref, right_ref, bias_ref, o_ref, v_ref, m_ref):
    blocks = groups * share
    width = bias_ref.shape[1]
    for a, ref in enumerate((left_ref, own_ref, right_ref)):
        for g in range(groups):
            for lb in range(share):
                part = ref[lb * CELLS : (lb + 1) * CELLS, g * width : (g + 1) * width]
                v_ref[a * blocks + g * share + lb] = part.astype(jnp.float32).reshape(64, 8, width)
    v_ref[3 * blocks] = jnp.zeros((64, 8, width), jnp.float32)
    bias = jnp.broadcast_to(bias_ref[...].astype(jnp.float32), (8, width))
    spans = (((0, 7),), tuple((t + 1, t) for t in range(8)), ((9, 0),))

    def one_block(b, carry):
        for dx in range(3):
            for dy in range(3):
                for dz in range(3):
                    slot = nb_ref[b, 9 * dx + 3 * dy + dz]
                    slot = jnp.where(slot < 0, 3 * blocks, slot)
                    for xd, xs in spans[dx]:
                        for yd, ys in spans[dy]:
                            row = 100 * xd + 10 * yd
                            if dz == 1:
                                m_ref[b, row + 1 : row + 9, :] = v_ref[slot, 8 * xs + ys]
                            else:
                                zd, zs = spans[dz][0]
                                m_ref[b, row + zd : row + zd + 1, :] = v_ref[slot, 8 * xs + ys, zs : zs + 1, :]
        m_ref[b, 1000:ROWS, :] = bias
        return carry

    lax.fori_loop(0, blocks, one_block, 0)
    for g in range(groups):
        for lb in range(share):
            o_ref[g, :, lb * width : (lb + 1) * width] = m_ref[g * share + lb].astype(jnp.bfloat16)


def build_margins(neighbors, left, own, right, bias, groups, share):
    width = bias.shape[1]
    blocks = groups * share
    vmem = pl.BlockSpec(memory_space=pltpu.VMEM)
    return pl.pallas_call(
        functools.partial(margin_kernel, groups, share),
        in_specs=[pl.BlockSpec(memory_space=pltpu.SMEM), vmem, vmem, vmem, vmem],
        out_specs=vmem,
        out_shape=jax.ShapeDtypeStruct((groups, ROWS, share * width), jnp.bfloat16),
        scratch_shapes=[
            pltpu.VMEM((3 * blocks + 1, 64, 8, width), jnp.float32),
            pltpu.VMEM((blocks, ROWS, width), jnp.float32),
        ],
        compiler_params=params(),
    )(neighbors, left, own, right, bias)


def conv_kernel(share, m_ref, w_ref, act_ref, o_ref, f_ref, q_ref):
    groups, _, width, outs = w_ref.shape
    wide = groups * width
    for lb in range(share):
        for g in range(groups):
            f_ref[lb, :, g * width : (g + 1) * width] = m_ref[g, :, lb * width : (lb + 1) * width].astype(jnp.float32)
    for k in range(3):
        for lb in range(share):
            for p in range(6):
                for y in range(10):
                    near = 100 * p + 10 * y + k
                    far = near + 400
                    q_ref[k, lb, p, y] = jnp.concatenate(
                        [f_ref[lb, near : near + 8, :], f_ref[lb, far : far + 8, :]], axis=0
                    ).astype(jnp.bfloat16)
    bias = f_ref[0, 1000:1001, :]
    for lb in range(share):
        total = None
        for k in range(3):
            windows, weights = [], []
            for i in range(3):
                for j in range(3):
                    windows.append(q_ref[k, lb, i : i + 4, j : j + 8].reshape(CELLS, wide))
                    for g in range(groups):
                        weights.append(w_ref[g, 9 * i + 3 * j + k])
            term = jnp.dot(
                jnp.concatenate(windows, axis=1),
                jnp.concatenate(weights, axis=0),
                preferred_element_type=jnp.float32,
            )
            total = term if total is None else total + term
        total = jnp.maximum(total + bias, 0.0).reshape(4, 8, 2, 8, outs)
        for h in range(2):
            half = total[:, :, h].reshape(256, outs).T
            seg = slice(lb * CELLS + h * 256, lb * CELLS + (h + 1) * 256)
            o_ref[:, seg] = (half * act_ref[:, seg]).astype(jnp.bfloat16)


def convolve(spread, weight_all, active, share):
    groups, _, width, outs = weight_all.shape
    vmem = pl.BlockSpec(memory_space=pltpu.VMEM)
    return pl.pallas_call(
        functools.partial(conv_kernel, share),
        in_specs=[vmem] * 3,
        out_specs=vmem,
        out_shape=jax.ShapeDtypeStruct((outs, share * CELLS), jnp.bfloat16),
        scratch_shapes=[
            pltpu.VMEM((share, ROWS, groups * width), jnp.float32),
            pltpu.VMEM((3, share, 6, 10, 16, groups * width), jnp.bfloat16),
        ],
        compiler_params=params(),
    )(spread, weight_all, active)


def pick_kernel(groups, v_ref, id_ref, o_ref, vox_ref):
    width, low_cells = v_ref.shape[0] // groups, v_ref.shape[1]
    rows = id_ref.shape[2]

    @pl.when(pl.program_id(0) == 0)
    def _():
        for g in range(groups):
            vox_ref[:, g * low_cells : (g + 1) * low_cells] = v_ref[g * width : (g + 1) * width, :]

    ids = id_ref[0]
    high = ids // low_cells
    low = ids % low_cells
    spots = lax.broadcasted_iota(jnp.int32, (low_cells, rows), 0)
    onehot = jnp.where(spots == low, 1.0, 0.0).astype(jnp.bfloat16)
    found = jnp.dot(v_ref[...], onehot, preferred_element_type=jnp.float32)
    total = jnp.zeros((width, rows), jnp.float32)
    for g in range(groups):
        total = jnp.where(jnp.broadcast_to(high, total.shape) == g, found[g * width : (g + 1) * width], total)
    o_ref[0] = total.astype(jnp.bfloat16)


def pick(parts, ids, owners, cap):
    groups, width, low_cells = parts.shape
    return pl.pallas_call(
        functools.partial(pick_kernel, groups),
        grid=(owners,),
        in_specs=[
            pl.BlockSpec((groups * width, low_cells), lambda s: (0, 0)),
            pl.BlockSpec((1, 1, cap), lambda s: (s, 0, 0)),
        ],
        out_specs=[
            pl.BlockSpec((1, width, cap), lambda s: (s, 0, 0)),
            pl.BlockSpec((width, groups * low_cells), lambda s: (0, 0)),
        ],
        out_shape=[
            jax.ShapeDtypeStruct((owners, width, cap), jnp.bfloat16),
            jax.ShapeDtypeStruct((width, groups * low_cells), jnp.bfloat16),
        ],
        compiler_params=params(),
    )(parts.reshape(groups * width, low_cells), ids.reshape(owners, 1, cap))


def add_kernel(p_ref, r_ref, o_ref):
    o_ref[...] = (p_ref[...].astype(jnp.float32) + r_ref[0].astype(jnp.float32)).astype(jnp.bfloat16)


def add_back(points, returned):
    owners, width, cap = returned.shape
    return pl.pallas_call(
        add_kernel,
        grid=(owners,),
        in_specs=[
            pl.BlockSpec((width, cap), lambda d: (0, d)),
            pl.BlockSpec((1, width, cap), lambda d: (d, 0, 0)),
        ],
        out_specs=pl.BlockSpec((width, cap), lambda d: (0, d)),
        out_shape=jax.ShapeDtypeStruct(points.shape, jnp.bfloat16),
        compiler_params=params(),
    )(points, returned)


def tally_cells(ids, cells):
    fine = 64
    high = (ids[None, :] // fine == jnp.arange(cells // fine, dtype=jnp.int32)[:, None]).astype(jnp.bfloat16)
    low = (ids[None, :] % fine == jnp.arange(fine, dtype=jnp.int32)[:, None]).astype(jnp.bfloat16)
    return lax.dot_general(high, low, (((1,), (1,)), ((), ())), preferred_element_type=jnp.float32).reshape(cells)


def on_device(points, point_cell, conv_weight, conv_bias, neighbors):
    width = points.shape[0]
    owners = lax.axis_size("space")
    groups = lax.axis_size("chan")
    cap = points.shape[2] // owners
    blocks = neighbors.shape[0]
    share = blocks // groups
    flat = points.reshape(width, owners * cap)
    ids = point_cell[0]
    weight_all = lax.all_gather(conv_weight, "chan", axis=0)
    counts = tally_cells(ids, blocks * CELLS)
    active = jnp.where(counts > 0.0, 1.0, 0.0).astype(jnp.float32)
    arrived = lax.all_to_all(split_slots(flat, owners, cap), "space", split_axis=0, concat_axis=0, tiled=True)
    own = pool(arrived, ids, counts, groups)
    left = lax.ppermute(own, "space", [(i, i + 1) for i in range(owners - 1)])
    right = lax.ppermute(own, "space", [(i + 1, i) for i in range(owners - 1)])
    margins = build_margins(neighbors, left, own, right, conv_bias.reshape(1, width), groups, share)
    spread = lax.all_to_all(margins, "chan", split_axis=0, concat_axis=0, tiled=True)
    mine = lax.dynamic_slice_in_dim(active, lax.axis_index("chan") * (share * CELLS), share * CELLS, 0)
    finished = convolve(spread, weight_all, mine.reshape(1, share * CELLS), share)
    finished = finished.reshape(groups, width, share * CELLS)
    parts = lax.all_to_all(finished, "chan", split_axis=0, concat_axis=0, tiled=True)
    picked, voxel_out = pick(parts, ids, owners, cap)
    returned = lax.all_to_all(picked, "space", split_axis=0, concat_axis=0, tiled=True)
    point_out = add_back(flat, returned).reshape(points.shape)
    return (voxel_out, point_out)


def solution(mesh):
    return jax.shard_map(
        on_device,
        mesh=mesh,
        in_specs=(
            P("chan", "space", None),
            P("space", None),
            P(None, "chan", None),
            P("chan"),
            P("space", None),
        ),
        out_specs=(P("chan", "space"), P("chan", "space", None)),
        check_vma=False,
    )
```

```python
import functools

import jax
import jax.numpy as jnp
from jax import lax
from jax.experimental import pallas as pl
from jax.experimental.pallas import tpu as pltpu
from jax.sharding import PartitionSpec as P

VMEM_LIMIT = 60 * 1024 * 1024
CELLS = 512
MESH = pl.DeviceIdType.MESH
ROWS = 1008


def params():
    return pltpu.CompilerParams(vmem_limit_bytes=VMEM_LIMIT)


def greet(axis, count):
    me = lax.axis_index(axis)
    barrier = pltpu.get_barrier_semaphore()

    def signal(t, carry):
        pl.semaphore_signal(barrier, inc=1, device_id={axis: lax.rem(me + t, count)}, device_id_type=MESH)
        return carry

    lax.fori_loop(1, count, signal, 0)
    pl.semaphore_wait(barrier, count - 1)
    return me


def remote_params(collective_id):
    return pltpu.CompilerParams(
        vmem_limit_bytes=VMEM_LIMIT, collective_id=collective_id, has_side_effects=True
    )


def pool_kernel(groups, low_cells, owners, x_ref, id_ref, count_ref, o_ref, held, acc_ref, send_sem, recv_sem, own_sem):
    width, rows = held.shape[1], held.shape[2]
    me = greet("space", owners)

    def chunk(d):
        return x_ref.at[:, pl.ds(pl.multiple_of(d * rows, rows), rows)]

    def copy(t):
        peer = lax.rem(me + t, owners)
        return pltpu.make_async_remote_copy(
            src_ref=chunk(peer),
            dst_ref=held.at[t],
            send_sem=send_sem.at[t],
            recv_sem=recv_sem.at[t],
            device_id={"space": peer},
            device_id_type=MESH,
        )

    def send(t, carry):
        copy(t).start()
        return carry

    lax.fori_loop(1, owners, send, 0)
    own = pltpu.make_async_copy(chunk(me), held.at[0], own_sem)
    own.start()
    acc_ref[...] = jnp.zeros_like(acc_ref)
    spots = lax.broadcasted_iota(jnp.int32, (low_cells, rows), 0)

    def add_chunk(t):
        ids = id_ref[lax.rem(me + owners - t, owners)]
        high = ids // low_cells
        low = ids % low_cells
        x = held[t]
        zero = jnp.zeros_like(x)
        masked = jnp.concatenate(
            [jnp.where(jnp.broadcast_to(high, x.shape) == g, x, zero) for g in range(groups)], axis=0
        )
        onehot = jnp.where(spots == low, 1.0, 0.0).astype(jnp.bfloat16)
        acc_ref[...] += lax.dot_general(
            onehot, masked, (((1,), (1,)), ((), ())), preferred_element_type=jnp.float32
        )

    own.wait()
    add_chunk(0)

    def take(t, carry):
        copy(t).wait_recv()
        add_chunk(t)
        return carry

    lax.fori_loop(1, owners, take, 0)
    for g in range(groups):
        lanes = slice(g * width, (g + 1) * width)
        tally = jnp.maximum(count_ref[:, g : g + 1], 1.0)
        o_ref[:, lanes] = (acc_ref[:, lanes] / tally).astype(jnp.bfloat16)

    def close(t, carry):
        copy(t).wait_send()
        return carry

    lax.fori_loop(1, owners, close, 0)


def pool(points, ids, counts, groups, owners, cap):
    width = points.shape[0]
    low_cells = counts.shape[0] // groups
    by_group = counts.reshape(groups, low_cells).T
    vmem = pl.BlockSpec(memory_space=pltpu.VMEM)
    return pl.pallas_call(
        functools.partial(pool_kernel, groups, low_cells, owners),
        in_specs=[pl.BlockSpec(memory_space=pl.ANY), vmem, vmem],
        out_specs=vmem,
        out_shape=jax.ShapeDtypeStruct((low_cells, groups * width), jnp.bfloat16),
        scratch_shapes=[
            pltpu.VMEM((owners, width, cap), jnp.bfloat16),
            pltpu.VMEM((low_cells, groups * width), jnp.float32),
            pltpu.SemaphoreType.DMA((owners,)),
            pltpu.SemaphoreType.DMA((owners,)),
            pltpu.SemaphoreType.DMA,
        ],
        compiler_params=remote_params(0),
    )(points, ids.reshape(owners, 1, cap), by_group)


def exchange_kernel(axis, count, x_ref, o_ref, send_sem, recv_sem):
    me = greet(axis, count)

    def copy(t, landing):
        peer = lax.rem(me + t, count)
        return pltpu.make_async_remote_copy(
            src_ref=x_ref.at[peer],
            dst_ref=o_ref.at[landing],
            send_sem=send_sem.at[t],
            recv_sem=recv_sem.at[t],
            device_id={axis: peer},
            device_id_type=MESH,
        )

    def send(t, carry):
        copy(t, me).start()
        return carry

    def close(t, carry):
        copy(t, lax.rem(me + count - t, count)).wait_recv()
        copy(t, me).wait_send()
        return carry

    lax.fori_loop(1, count, send, 0)
    o_ref[me] = x_ref[me]
    lax.fori_loop(1, count, close, 0)


def exchange(x, axis, collective_id):
    count = lax.axis_size(axis)
    vmem = pl.BlockSpec(memory_space=pltpu.VMEM)
    return pl.pallas_call(
        functools.partial(exchange_kernel, axis, count),
        in_specs=[vmem],
        out_specs=vmem,
        out_shape=jax.ShapeDtypeStruct(x.shape, x.dtype),
        scratch_shapes=[pltpu.SemaphoreType.DMA((count,)), pltpu.SemaphoreType.DMA((count,))],
        compiler_params=remote_params(collective_id),
    )(x)


def margin_kernel(groups, share, nb_ref, left_ref, own_ref, right_ref, bias_ref, o_ref, v_ref, m_ref):
    blocks = groups * share
    width = bias_ref.shape[1]
    for a, ref in enumerate((left_ref, own_ref, right_ref)):
        for g in range(groups):
            for lb in range(share):
                part = ref[lb * CELLS : (lb + 1) * CELLS, g * width : (g + 1) * width]
                v_ref[a * blocks + g * share + lb] = part.astype(jnp.float32).reshape(64, 8, width)
    v_ref[3 * blocks] = jnp.zeros((64, 8, width), jnp.float32)
    bias = jnp.broadcast_to(bias_ref[...].astype(jnp.float32), (8, width))
    spans = (((0, 7),), tuple((t + 1, t) for t in range(8)), ((9, 0),))

    def one_block(b, carry):
        for dx in range(3):
            for dy in range(3):
                for dz in range(3):
                    slot = nb_ref[b, 9 * dx + 3 * dy + dz]
                    slot = jnp.where(slot < 0, 3 * blocks, slot)
                    for xd, xs in spans[dx]:
                        for yd, ys in spans[dy]:
                            row = 100 * xd + 10 * yd
                            if dz == 1:
                                m_ref[b, row + 1 : row + 9, :] = v_ref[slot, 8 * xs + ys]
                            else:
                                zd, zs = spans[dz][0]
                                m_ref[b, row + zd : row + zd + 1, :] = v_ref[slot, 8 * xs + ys, zs : zs + 1, :]
        m_ref[b, 1000:ROWS, :] = bias
        return carry

    lax.fori_loop(0, blocks, one_block, 0)
    for g in range(groups):
        for lb in range(share):
            o_ref[g, :, lb * width : (lb + 1) * width] = m_ref[g * share + lb].astype(jnp.bfloat16)


def build_margins(neighbors, left, own, right, bias, groups, share):
    width = bias.shape[1]
    blocks = groups * share
    vmem = pl.BlockSpec(memory_space=pltpu.VMEM)
    return pl.pallas_call(
        functools.partial(margin_kernel, groups, share),
        in_specs=[pl.BlockSpec(memory_space=pltpu.SMEM), vmem, vmem, vmem, vmem],
        out_specs=vmem,
        out_shape=jax.ShapeDtypeStruct((groups, ROWS, share * width), jnp.bfloat16),
        scratch_shapes=[
            pltpu.VMEM((3 * blocks + 1, 64, 8, width), jnp.float32),
            pltpu.VMEM((blocks, ROWS, width), jnp.float32),
        ],
        compiler_params=params(),
    )(neighbors, left, own, right, bias)


def conv_kernel(share, m_ref, w_ref, act_ref, o_ref, f_ref, q_ref):
    groups, _, width, outs = w_ref.shape
    wide = groups * width
    for lb in range(share):
        for g in range(groups):
            f_ref[lb, :, g * width : (g + 1) * width] = m_ref[g, :, lb * width : (lb + 1) * width].astype(jnp.float32)
    for k in range(3):
        for lb in range(share):
            for p in range(6):
                for y in range(10):
                    near = 100 * p + 10 * y + k
                    far = near + 400
                    q_ref[k, lb, p, y] = jnp.concatenate(
                        [f_ref[lb, near : near + 8, :], f_ref[lb, far : far + 8, :]], axis=0
                    ).astype(jnp.bfloat16)
    bias = f_ref[0, 1000:1001, :]
    for lb in range(share):
        total = None
        for k in range(3):
            windows, weights = [], []
            for i in range(3):
                for j in range(3):
                    windows.append(q_ref[k, lb, i : i + 4, j : j + 8].reshape(CELLS, wide))
                    for g in range(groups):
                        weights.append(w_ref[g, 9 * i + 3 * j + k])
            term = jnp.dot(
                jnp.concatenate(windows, axis=1),
                jnp.concatenate(weights, axis=0),
                preferred_element_type=jnp.float32,
            )
            total = term if total is None else total + term
        total = jnp.maximum(total + bias, 0.0).reshape(4, 8, 2, 8, outs)
        for h in range(2):
            half = total[:, :, h].reshape(256, outs).T
            seg = slice(lb * CELLS + h * 256, lb * CELLS + (h + 1) * 256)
            o_ref[:, seg] = (half * act_ref[:, seg]).astype(jnp.bfloat16)


def convolve(spread, weight_all, active, share):
    groups, _, width, outs = weight_all.shape
    vmem = pl.BlockSpec(memory_space=pltpu.VMEM)
    return pl.pallas_call(
        functools.partial(conv_kernel, share),
        in_specs=[vmem] * 3,
        out_specs=vmem,
        out_shape=jax.ShapeDtypeStruct((outs, share * CELLS), jnp.bfloat16),
        scratch_shapes=[
            pltpu.VMEM((share, ROWS, groups * width), jnp.float32),
            pltpu.VMEM((3, share, 6, 10, 16, groups * width), jnp.bfloat16),
        ],
        compiler_params=params(),
    )(spread, weight_all, active)


def return_kernel(groups, owners, v_ref, id_ref, p_ref, o_ref, found_ref, held, send_sem, recv_sem):
    width, low_cells = v_ref.shape[0] // groups, v_ref.shape[1]
    rows = id_ref.shape[2]
    me = greet("space", owners)
    spots = lax.broadcasted_iota(jnp.int32, (low_cells, rows), 0)

    def copy(t):
        return pltpu.make_async_remote_copy(
            src_ref=found_ref.at[t],
            dst_ref=held.at[t],
            send_sem=send_sem.at[t],
            recv_sem=recv_sem.at[t],
            device_id={"space": lax.rem(me + t, owners)},
            device_id_type=MESH,
        )

    def pick(s):
        ids = id_ref[s]
        high = ids // low_cells
        low = ids % low_cells
        onehot = jnp.where(spots == low, 1.0, 0.0).astype(jnp.bfloat16)
        found = jnp.dot(v_ref[...], onehot, preferred_element_type=jnp.float32)
        total = jnp.zeros((width, rows), jnp.float32)
        for g in range(groups):
            total = jnp.where(jnp.broadcast_to(high, total.shape) == g, found[g * width : (g + 1) * width], total)
        return total

    def add(d, values):
        at = pl.ds(pl.multiple_of(d * rows, rows), rows)
        o_ref[:, at] = (p_ref[:, at].astype(jnp.float32) + values).astype(jnp.bfloat16)

    def send(t, carry):
        found_ref[t] = pick(lax.rem(me + t, owners)).astype(jnp.bfloat16)
        copy(t).start()
        return carry

    def take(t, carry):
        copy(t).wait_recv()
        add(lax.rem(me + owners - t, owners), held[t].astype(jnp.float32))
        return carry

    def close(t, carry):
        copy(t).wait_send()
        return carry

    lax.fori_loop(1, owners, send, 0)
    add(me, pick(me))
    lax.fori_loop(1, owners, take, 0)
    lax.fori_loop(1, owners, close, 0)


def give_back(parts, ids, points, owners, cap):
    groups, width, low_cells = parts.shape
    vmem = pl.BlockSpec(memory_space=pltpu.VMEM)
    return pl.pallas_call(
        functools.partial(return_kernel, groups, owners),
        in_specs=[vmem] * 3,
        out_specs=vmem,
        out_shape=jax.ShapeDtypeStruct(points.shape, jnp.bfloat16),
        scratch_shapes=[
            pltpu.VMEM((owners, width, cap), jnp.bfloat16),
            pltpu.VMEM((owners, width, cap), jnp.bfloat16),
            pltpu.SemaphoreType.DMA((owners,)),
            pltpu.SemaphoreType.DMA((owners,)),
        ],
        compiler_params=remote_params(3),
    )(parts.reshape(groups * width, low_cells), ids.reshape(owners, 1, cap), points)


def tally_cells(ids, cells):
    fine = 64
    high = (ids[None, :] // fine == jnp.arange(cells // fine, dtype=jnp.int32)[:, None]).astype(jnp.bfloat16)
    low = (ids[None, :] % fine == jnp.arange(fine, dtype=jnp.int32)[:, None]).astype(jnp.bfloat16)
    return lax.dot_general(high, low, (((1,), (1,)), ((), ())), preferred_element_type=jnp.float32).reshape(cells)


def on_device(points, point_cell, conv_weight, conv_bias, neighbors):
    width = points.shape[0]
    owners = lax.axis_size("space")
    groups = lax.axis_size("chan")
    cap = points.shape[2] // owners
    blocks = neighbors.shape[0]
    share = blocks // groups
    flat = points.reshape(width, owners * cap)
    ids = point_cell[0]
    weight_all = lax.all_gather(conv_weight, "chan", axis=0)
    counts = tally_cells(ids, blocks * CELLS)
    active = jnp.where(counts > 0.0, 1.0, 0.0).astype(jnp.float32)
    own = pool(flat, ids, counts, groups, owners, cap)
    left = lax.ppermute(own, "space", [(i, i + 1) for i in range(owners - 1)])
    right = lax.ppermute(own, "space", [(i + 1, i) for i in range(owners - 1)])
    margins = build_margins(neighbors, left, own, right, conv_bias.reshape(1, width), groups, share)
    spread = exchange(margins, "chan", 1)
    mine = lax.dynamic_slice_in_dim(active, lax.axis_index("chan") * (share * CELLS), share * CELLS, 0)
    finished = convolve(spread, weight_all, mine.reshape(1, share * CELLS), share)
    finished = finished.reshape(groups, width, share * CELLS)
    parts = exchange(finished, "chan", 2)
    voxel_out = jnp.transpose(parts, (1, 0, 2)).reshape(width, blocks * CELLS)
    point_out = give_back(parts, ids, flat, owners, cap).reshape(points.shape)
    return (voxel_out, point_out)


def solution(mesh):
    return jax.shard_map(
        on_device,
        mesh=mesh,
        in_specs=(
            P("chan", "space", None),
            P("space", None),
            P(None, "chan", None),
            P("chan"),
            P("space", None),
        ),
        out_specs=(P("chan", "space"), P("chan", "space", None)),
        check_vma=False,
    )
```

```python
import functools

import jax
import jax.numpy as jnp
from jax import lax
from jax.experimental import pallas as pl
from jax.experimental.pallas import tpu as pltpu
from jax.sharding import PartitionSpec as P

VMEM_LIMIT = 60 * 1024 * 1024
CELLS = 512
MESH = pl.DeviceIdType.MESH
ROWS = 1008


def params():
    return pltpu.CompilerParams(vmem_limit_bytes=VMEM_LIMIT)


def greet(axis, count):
    me = lax.axis_index(axis)
    barrier = pltpu.get_barrier_semaphore()

    def signal(t, carry):
        pl.semaphore_signal(barrier, inc=1, device_id={axis: lax.rem(me + t, count)}, device_id_type=MESH)
        return carry

    lax.fori_loop(1, count, signal, 0)
    pl.semaphore_wait(barrier, count - 1)
    return me


def remote_params(collective_id):
    return pltpu.CompilerParams(
        vmem_limit_bytes=VMEM_LIMIT, collective_id=collective_id, has_side_effects=True
    )


def pool_kernel(groups, low_cells, owners, x_ref, id_ref, count_ref, o_ref, held, acc_ref, send_sem, recv_sem, own_sem):
    width, rows = held.shape[1], held.shape[2]
    me = greet("space", owners)

    def chunk(d):
        return x_ref.at[:, pl.ds(pl.multiple_of(d * rows, rows), rows)]

    def copy(t):
        peer = lax.rem(me + t, owners)
        return pltpu.make_async_remote_copy(
            src_ref=chunk(peer),
            dst_ref=held.at[t],
            send_sem=send_sem.at[t],
            recv_sem=recv_sem.at[t],
            device_id={"space": peer},
            device_id_type=MESH,
        )

    def send(t, carry):
        copy(t).start()
        return carry

    lax.fori_loop(1, owners, send, 0)
    own = pltpu.make_async_copy(chunk(me), held.at[0], own_sem)
    own.start()
    acc_ref[...] = jnp.zeros_like(acc_ref)
    spots = lax.broadcasted_iota(jnp.int32, (low_cells, rows), 0)

    def add_chunk(t):
        ids = id_ref[lax.rem(me + owners - t, owners)]
        high = ids // low_cells
        low = ids % low_cells
        x = held[t]
        zero = jnp.zeros_like(x)
        masked = jnp.concatenate(
            [jnp.where(jnp.broadcast_to(high, x.shape) == g, x, zero) for g in range(groups)], axis=0
        )
        onehot = jnp.where(spots == low, 1.0, 0.0).astype(jnp.bfloat16)
        acc_ref[...] += lax.dot_general(
            onehot, masked, (((1,), (1,)), ((), ())), preferred_element_type=jnp.float32
        )

    own.wait()
    add_chunk(0)

    def take(t, carry):
        copy(t).wait_recv()
        add_chunk(t)
        return carry

    lax.fori_loop(1, owners, take, 0)
    for g in range(groups):
        lanes = slice(g * width, (g + 1) * width)
        tally = jnp.maximum(count_ref[:, g : g + 1], 1.0)
        o_ref[:, lanes] = (acc_ref[:, lanes] / tally).astype(jnp.bfloat16)

    def close(t, carry):
        copy(t).wait_send()
        return carry

    lax.fori_loop(1, owners, close, 0)


def pool(points, ids, counts, groups, owners, cap):
    width = points.shape[0]
    low_cells = counts.shape[0] // groups
    by_group = counts.reshape(groups, low_cells).T
    vmem = pl.BlockSpec(memory_space=pltpu.VMEM)
    return pl.pallas_call(
        functools.partial(pool_kernel, groups, low_cells, owners),
        in_specs=[pl.BlockSpec(memory_space=pl.ANY), vmem, vmem],
        out_specs=vmem,
        out_shape=jax.ShapeDtypeStruct((low_cells, groups * width), jnp.bfloat16),
        scratch_shapes=[
            pltpu.VMEM((owners, width, cap), jnp.bfloat16),
            pltpu.VMEM((low_cells, groups * width), jnp.float32),
            pltpu.SemaphoreType.DMA((owners,)),
            pltpu.SemaphoreType.DMA((owners,)),
            pltpu.SemaphoreType.DMA,
        ],
        compiler_params=remote_params(0),
    )(points, ids.reshape(owners, 1, cap), by_group)


def exchange_kernel(axis, count, x_ref, o_ref, send_sem, recv_sem):
    me = greet(axis, count)

    def copy(t, landing):
        peer = lax.rem(me + t, count)
        return pltpu.make_async_remote_copy(
            src_ref=x_ref.at[peer],
            dst_ref=o_ref.at[landing],
            send_sem=send_sem.at[t],
            recv_sem=recv_sem.at[t],
            device_id={axis: peer},
            device_id_type=MESH,
        )

    def send(t, carry):
        copy(t, me).start()
        return carry

    def close(t, carry):
        copy(t, lax.rem(me + count - t, count)).wait_recv()
        copy(t, me).wait_send()
        return carry

    lax.fori_loop(1, count, send, 0)
    o_ref[me] = x_ref[me]
    lax.fori_loop(1, count, close, 0)


def exchange(x, axis, collective_id):
    count = lax.axis_size(axis)
    vmem = pl.BlockSpec(memory_space=pltpu.VMEM)
    return pl.pallas_call(
        functools.partial(exchange_kernel, axis, count),
        in_specs=[vmem],
        out_specs=vmem,
        out_shape=jax.ShapeDtypeStruct(x.shape, x.dtype),
        scratch_shapes=[pltpu.SemaphoreType.DMA((count,)), pltpu.SemaphoreType.DMA((count,))],
        compiler_params=remote_params(collective_id),
    )(x)


def margin_kernel(groups, share, nb_ref, left_ref, own_ref, right_ref, bias_ref, o_ref, v_ref, m_ref):
    blocks = groups * share
    width = bias_ref.shape[1]
    for a, ref in enumerate((left_ref, own_ref, right_ref)):
        for g in range(groups):
            for lb in range(share):
                part = ref[lb * CELLS : (lb + 1) * CELLS, g * width : (g + 1) * width]
                v_ref[a * blocks + g * share + lb] = part.astype(jnp.float32).reshape(64, 8, width)
    v_ref[3 * blocks] = jnp.zeros((64, 8, width), jnp.float32)
    bias = jnp.broadcast_to(bias_ref[...].astype(jnp.float32), (8, width))
    spans = (((0, 7),), tuple((t + 1, t) for t in range(8)), ((9, 0),))

    def one_block(b, carry):
        for dx in range(3):
            for dy in range(3):
                for dz in range(3):
                    slot = nb_ref[b, 9 * dx + 3 * dy + dz]
                    slot = jnp.where(slot < 0, 3 * blocks, slot)
                    for xd, xs in spans[dx]:
                        for yd, ys in spans[dy]:
                            row = 100 * xd + 10 * yd
                            if dz == 1:
                                m_ref[b, row + 1 : row + 9, :] = v_ref[slot, 8 * xs + ys]
                            else:
                                zd, zs = spans[dz][0]
                                m_ref[b, row + zd : row + zd + 1, :] = v_ref[slot, 8 * xs + ys, zs : zs + 1, :]
        m_ref[b, 1000:ROWS, :] = bias
        return carry

    lax.fori_loop(0, blocks, one_block, 0)
    for g in range(groups):
        for lb in range(share):
            o_ref[g, :, lb * width : (lb + 1) * width] = m_ref[g * share + lb].astype(jnp.bfloat16)


def build_margins(neighbors, left, own, right, bias, groups, share):
    width = bias.shape[1]
    blocks = groups * share
    vmem = pl.BlockSpec(memory_space=pltpu.VMEM)
    return pl.pallas_call(
        functools.partial(margin_kernel, groups, share),
        in_specs=[pl.BlockSpec(memory_space=pltpu.SMEM), vmem, vmem, vmem, vmem],
        out_specs=vmem,
        out_shape=jax.ShapeDtypeStruct((groups, ROWS, share * width), jnp.bfloat16),
        scratch_shapes=[
            pltpu.VMEM((3 * blocks + 1, 64, 8, width), jnp.float32),
            pltpu.VMEM((blocks, ROWS, width), jnp.float32),
        ],
        compiler_params=params(),
    )(neighbors, left, own, right, bias)


def conv_kernel(share, m_ref, w_ref, act_ref, o_ref, f_ref, q_ref):
    halves, groups, _, part, outs = w_ref.shape
    width = halves * part
    wide = groups * width
    for lb in range(share):
        for g in range(groups):
            f_ref[lb, :, g * width : (g + 1) * width] = m_ref[g, :, lb * width : (lb + 1) * width].astype(jnp.float32)
    for k in range(3):
        for lb in range(share):
            for p in range(6):
                for y in range(10):
                    near = 100 * p + 10 * y + k
                    far = near + 400
                    q_ref[k, lb, p, y] = jnp.concatenate(
                        [f_ref[lb, near : near + 8, :], f_ref[lb, far : far + 8, :]], axis=0
                    ).astype(jnp.bfloat16)
    bias = f_ref[0, 1000:1001, :]
    for lb in range(share):
        total = None
        for k in range(3):
            windows, weights = [], []
            for i in range(3):
                for j in range(3):
                    windows.append(q_ref[k, lb, i : i + 4, j : j + 8].reshape(CELLS, wide))
                    for g in range(groups):
                        for half in range(halves):
                            weights.append(w_ref[half, g, 9 * i + 3 * j + k])
            term = jnp.dot(
                jnp.concatenate(windows, axis=1),
                jnp.concatenate(weights, axis=0),
                preferred_element_type=jnp.float32,
            )
            total = term if total is None else total + term
        total = jnp.maximum(total + bias, 0.0).reshape(4, 8, 2, 8, outs)
        for h in range(2):
            half = total[:, :, h].reshape(256, outs).T
            seg = slice(lb * CELLS + h * 256, lb * CELLS + (h + 1) * 256)
            o_ref[:, seg] = (half * act_ref[:, seg]).astype(jnp.bfloat16)


def convolve(spread, weight_all, active, share):
    halves, groups, _, part, outs = weight_all.shape
    vmem = pl.BlockSpec(memory_space=pltpu.VMEM)
    return pl.pallas_call(
        functools.partial(conv_kernel, share),
        in_specs=[vmem] * 3,
        out_specs=vmem,
        out_shape=jax.ShapeDtypeStruct((outs, share * CELLS), jnp.bfloat16),
        scratch_shapes=[
            pltpu.VMEM((share, ROWS, groups * halves * part), jnp.float32),
            pltpu.VMEM((3, share, 6, 10, 16, groups * halves * part), jnp.bfloat16),
        ],
        compiler_params=params(),
    )(spread, weight_all, active)


def return_kernel(groups, owners, v_ref, id_ref, p_ref, o_ref, found_ref, held, send_sem, recv_sem):
    width, low_cells = v_ref.shape[0] // groups, v_ref.shape[1]
    rows = id_ref.shape[2]
    me = greet("space", owners)
    spots = lax.broadcasted_iota(jnp.int32, (low_cells, rows), 0)

    def copy(t):
        return pltpu.make_async_remote_copy(
            src_ref=found_ref.at[t],
            dst_ref=held.at[t],
            send_sem=send_sem.at[t],
            recv_sem=recv_sem.at[t],
            device_id={"space": lax.rem(me + t, owners)},
            device_id_type=MESH,
        )

    def pick(s):
        ids = id_ref[s]
        high = ids // low_cells
        low = ids % low_cells
        onehot = jnp.where(spots == low, 1.0, 0.0).astype(jnp.bfloat16)
        found = jnp.dot(v_ref[...], onehot, preferred_element_type=jnp.float32)
        total = jnp.zeros((width, rows), jnp.float32)
        for g in range(groups):
            total = jnp.where(jnp.broadcast_to(high, total.shape) == g, found[g * width : (g + 1) * width], total)
        return total

    def add(d, values):
        at = pl.ds(pl.multiple_of(d * rows, rows), rows)
        o_ref[:, at] = (p_ref[:, at].astype(jnp.float32) + values).astype(jnp.bfloat16)

    def send(t, carry):
        found_ref[t] = pick(lax.rem(me + t, owners)).astype(jnp.bfloat16)
        copy(t).start()
        return carry

    def take(t, carry):
        copy(t).wait_recv()
        add(lax.rem(me + owners - t, owners), held[t].astype(jnp.float32))
        return carry

    def close(t, carry):
        copy(t).wait_send()
        return carry

    lax.fori_loop(1, owners, send, 0)
    add(me, pick(me))
    lax.fori_loop(1, owners, take, 0)
    lax.fori_loop(1, owners, close, 0)


def give_back(parts, ids, points, owners, cap):
    groups, width, low_cells = parts.shape
    vmem = pl.BlockSpec(memory_space=pltpu.VMEM)
    return pl.pallas_call(
        functools.partial(return_kernel, groups, owners),
        in_specs=[vmem] * 3,
        out_specs=vmem,
        out_shape=jax.ShapeDtypeStruct(points.shape, jnp.bfloat16),
        scratch_shapes=[
            pltpu.VMEM((owners, width, cap), jnp.bfloat16),
            pltpu.VMEM((owners, width, cap), jnp.bfloat16),
            pltpu.SemaphoreType.DMA((owners,)),
            pltpu.SemaphoreType.DMA((owners,)),
        ],
        compiler_params=remote_params(3),
    )(parts.reshape(groups * width, low_cells), ids.reshape(owners, 1, cap), points)


def tally_cells(ids, cells):
    fine = 64
    high = (ids[None, :] // fine == jnp.arange(cells // fine, dtype=jnp.int32)[:, None]).astype(jnp.bfloat16)
    low = (ids[None, :] % fine == jnp.arange(fine, dtype=jnp.int32)[:, None]).astype(jnp.bfloat16)
    return lax.dot_general(high, low, (((1,), (1,)), ((), ())), preferred_element_type=jnp.float32).reshape(cells)


def gather_half(conv_weight):
    half = conv_weight.shape[1] // 2
    mine = lax.dynamic_slice_in_dim(conv_weight, lax.rem(lax.axis_index("space"), 2) * half, half, 1)
    return lax.all_gather(mine, "chan", axis=0)


def swap_halves(gathered, owners):
    pairs = [[i, i + 1] for i in range(0, owners, 2)]
    return lax.all_gather(gathered, "space", axis=0, axis_index_groups=pairs)


def on_device(points, point_cell, conv_weight, conv_bias, neighbors):
    width = points.shape[0]
    owners = lax.axis_size("space")
    groups = lax.axis_size("chan")
    cap = points.shape[2] // owners
    blocks = neighbors.shape[0]
    share = blocks // groups
    flat = points.reshape(width, owners * cap)
    ids = point_cell[0]
    gathered = gather_half(conv_weight)
    counts = tally_cells(ids, blocks * CELLS)
    active = jnp.where(counts > 0.0, 1.0, 0.0).astype(jnp.float32)
    own = pool(flat, ids, counts, groups, owners, cap)
    gathered, own = lax.optimization_barrier((gathered, own))
    weight_all = swap_halves(gathered, owners)
    left = lax.ppermute(own, "space", [(i, i + 1) for i in range(owners - 1)])
    right = lax.ppermute(own, "space", [(i + 1, i) for i in range(owners - 1)])
    margins = build_margins(neighbors, left, own, right, conv_bias.reshape(1, width), groups, share)
    spread = exchange(margins, "chan", 1)
    mine = lax.dynamic_slice_in_dim(active, lax.axis_index("chan") * (share * CELLS), share * CELLS, 0)
    finished = convolve(spread, weight_all, mine.reshape(1, share * CELLS), share)
    finished = finished.reshape(groups, width, share * CELLS)
    parts = exchange(finished, "chan", 2)
    voxel_out = jnp.transpose(parts, (1, 0, 2)).reshape(width, blocks * CELLS)
    point_out = give_back(parts, ids, flat, owners, cap).reshape(points.shape)
    return (voxel_out, point_out)


def solution(mesh):
    return jax.shard_map(
        on_device,
        mesh=mesh,
        in_specs=(
            P("chan", "space", None),
            P("space", None),
            P(None, "chan", None),
            P("chan"),
            P("space", None),
        ),
        out_specs=(P("chan", "space"), P("chan", "space", None)),
        check_vma=False,
    )
```

```python
import functools

import jax
import jax.numpy as jnp
from jax import lax
from jax.experimental import pallas as pl
from jax.experimental.pallas import tpu as pltpu
from jax.sharding import PartitionSpec as P

VMEM_LIMIT = 60 * 1024 * 1024
CELLS = 512
MESH = pl.DeviceIdType.MESH
ROWS = 1008


def params():
    return pltpu.CompilerParams(vmem_limit_bytes=VMEM_LIMIT)


def greet(axis, count):
    me = lax.axis_index(axis)
    barrier = pltpu.get_barrier_semaphore()

    def signal(t, carry):
        pl.semaphore_signal(barrier, inc=1, device_id={axis: lax.rem(me + t, count)}, device_id_type=MESH)
        return carry

    lax.fori_loop(1, count, signal, 0)
    pl.semaphore_wait(barrier, count - 1)
    return me


def remote_params(collective_id):
    return pltpu.CompilerParams(
        vmem_limit_bytes=VMEM_LIMIT, collective_id=collective_id, has_side_effects=True
    )


def pool_kernel(groups, low_cells, owners, x_ref, id_ref, count_ref, o_ref, held, acc_ref, send_sem, recv_sem, own_sem):
    width, rows = held.shape[1], held.shape[2]
    me = greet("space", owners)

    def chunk(d):
        return x_ref.at[:, pl.ds(pl.multiple_of(d * rows, rows), rows)]

    def copy(t):
        peer = lax.rem(me + t, owners)
        return pltpu.make_async_remote_copy(
            src_ref=chunk(peer),
            dst_ref=held.at[t],
            send_sem=send_sem.at[t],
            recv_sem=recv_sem.at[t],
            device_id={"space": peer},
            device_id_type=MESH,
        )

    def send(t, carry):
        copy(t).start()
        return carry

    lax.fori_loop(1, owners, send, 0)
    own = pltpu.make_async_copy(chunk(me), held.at[0], own_sem)
    own.start()
    acc_ref[...] = jnp.zeros_like(acc_ref)
    spots = lax.broadcasted_iota(jnp.int32, (low_cells, rows), 0)

    def add_chunk(t):
        ids = id_ref[lax.rem(me + owners - t, owners)]
        high = ids // low_cells
        low = ids % low_cells
        x = held[t]
        zero = jnp.zeros_like(x)
        masked = jnp.concatenate(
            [jnp.where(jnp.broadcast_to(high, x.shape) == g, x, zero) for g in range(groups)], axis=0
        )
        onehot = jnp.where(spots == low, 1.0, 0.0).astype(jnp.bfloat16)
        acc_ref[...] += lax.dot_general(
            onehot, masked, (((1,), (1,)), ((), ())), preferred_element_type=jnp.float32
        )

    own.wait()
    add_chunk(0)

    def take(t, carry):
        copy(t).wait_recv()
        add_chunk(t)
        return carry

    lax.fori_loop(1, owners, take, 0)
    for g in range(groups):
        lanes = slice(g * width, (g + 1) * width)
        tally = jnp.maximum(count_ref[:, g : g + 1], 1.0)
        o_ref[:, lanes] = (acc_ref[:, lanes] / tally).astype(jnp.bfloat16)

    def close(t, carry):
        copy(t).wait_send()
        return carry

    lax.fori_loop(1, owners, close, 0)


def pool(points, ids, counts, groups, owners, cap):
    width = points.shape[0]
    low_cells = counts.shape[0] // groups
    by_group = counts.reshape(groups, low_cells).T
    vmem = pl.BlockSpec(memory_space=pltpu.VMEM)
    return pl.pallas_call(
        functools.partial(pool_kernel, groups, low_cells, owners),
        in_specs=[pl.BlockSpec(memory_space=pl.ANY), vmem, vmem],
        out_specs=vmem,
        out_shape=jax.ShapeDtypeStruct((low_cells, groups * width), jnp.bfloat16),
        scratch_shapes=[
            pltpu.VMEM((owners, width, cap), jnp.bfloat16),
            pltpu.VMEM((low_cells, groups * width), jnp.float32),
            pltpu.SemaphoreType.DMA((owners,)),
            pltpu.SemaphoreType.DMA((owners,)),
            pltpu.SemaphoreType.DMA,
        ],
        compiler_params=remote_params(0),
    )(points, ids.reshape(owners, 1, cap), by_group)


def exchange_kernel(axis, count, x_ref, o_ref, send_sem, recv_sem):
    me = greet(axis, count)

    def copy(t, landing):
        peer = lax.rem(me + t, count)
        return pltpu.make_async_remote_copy(
            src_ref=x_ref.at[peer],
            dst_ref=o_ref.at[landing],
            send_sem=send_sem.at[t],
            recv_sem=recv_sem.at[t],
            device_id={axis: peer},
            device_id_type=MESH,
        )

    def send(t, carry):
        copy(t, me).start()
        return carry

    def close(t, carry):
        copy(t, lax.rem(me + count - t, count)).wait_recv()
        copy(t, me).wait_send()
        return carry

    lax.fori_loop(1, count, send, 0)
    o_ref[me] = x_ref[me]
    lax.fori_loop(1, count, close, 0)


def exchange(x, axis, collective_id):
    count = lax.axis_size(axis)
    vmem = pl.BlockSpec(memory_space=pltpu.VMEM)
    return pl.pallas_call(
        functools.partial(exchange_kernel, axis, count),
        in_specs=[vmem],
        out_specs=vmem,
        out_shape=jax.ShapeDtypeStruct(x.shape, x.dtype),
        scratch_shapes=[pltpu.SemaphoreType.DMA((count,)), pltpu.SemaphoreType.DMA((count,))],
        compiler_params=remote_params(collective_id),
    )(x)


def margin_kernel(groups, share, nb_ref, left_ref, own_ref, right_ref, bias_ref, o_ref, v_ref, m_ref):
    blocks = groups * share
    width = bias_ref.shape[1]
    for a, ref in enumerate((left_ref, own_ref, right_ref)):
        for g in range(groups):
            for lb in range(share):
                part = ref[lb * CELLS : (lb + 1) * CELLS, g * width : (g + 1) * width]
                v_ref[a * blocks + g * share + lb] = part.astype(jnp.float32).reshape(64, 8, width)
    v_ref[3 * blocks] = jnp.zeros((64, 8, width), jnp.float32)
    bias = jnp.broadcast_to(bias_ref[...].astype(jnp.float32), (8, width))
    spans = (((0, 7),), tuple((t + 1, t) for t in range(8)), ((9, 0),))

    def one_block(b, carry):
        for dx in range(3):
            for dy in range(3):
                for dz in range(3):
                    slot = nb_ref[b, 9 * dx + 3 * dy + dz]
                    slot = jnp.where(slot < 0, 3 * blocks, slot)
                    for xd, xs in spans[dx]:
                        for yd, ys in spans[dy]:
                            row = 100 * xd + 10 * yd
                            if dz == 1:
                                m_ref[b, row + 1 : row + 9, :] = v_ref[slot, 8 * xs + ys]
                            else:
                                zd, zs = spans[dz][0]
                                m_ref[b, row + zd : row + zd + 1, :] = v_ref[slot, 8 * xs + ys, zs : zs + 1, :]
        m_ref[b, 1000:ROWS, :] = bias
        return carry

    lax.fori_loop(0, blocks, one_block, 0)
    for g in range(groups):
        for lb in range(share):
            o_ref[g, :, lb * width : (lb + 1) * width] = m_ref[g * share + lb].astype(jnp.bfloat16)


def build_margins(neighbors, left, own, right, bias, groups, share):
    width = bias.shape[1]
    blocks = groups * share
    vmem = pl.BlockSpec(memory_space=pltpu.VMEM)
    return pl.pallas_call(
        functools.partial(margin_kernel, groups, share),
        in_specs=[pl.BlockSpec(memory_space=pltpu.SMEM), vmem, vmem, vmem, vmem],
        out_specs=vmem,
        out_shape=jax.ShapeDtypeStruct((groups, ROWS, share * width), jnp.bfloat16),
        scratch_shapes=[
            pltpu.VMEM((3 * blocks + 1, 64, 8, width), jnp.float32),
            pltpu.VMEM((blocks, ROWS, width), jnp.float32),
        ],
        compiler_params=params(),
    )(neighbors, left, own, right, bias)


def conv_kernel(share, m_ref, w_ref, act_ref, o_ref, f_ref, q_ref):
    halves, groups, _, part, outs = w_ref.shape
    width = halves * part
    wide = groups * width
    for lb in range(share):
        for g in range(groups):
            f_ref[lb, :, g * width : (g + 1) * width] = m_ref[g, :, lb * width : (lb + 1) * width].astype(jnp.float32)
    for k in range(3):
        for lb in range(share):
            for p in range(6):
                for y in range(10):
                    near = 100 * p + 10 * y + k
                    far = near + 400
                    q_ref[k, lb, p, y] = jnp.concatenate(
                        [f_ref[lb, near : near + 8, :], f_ref[lb, far : far + 8, :]], axis=0
                    ).astype(jnp.bfloat16)
    bias = f_ref[0, 1000:1001, :]
    for lb in range(share):
        total = None
        for k in range(3):
            windows, weights = [], []
            for i in range(3):
                for j in range(3):
                    windows.append(q_ref[k, lb, i : i + 4, j : j + 8].reshape(CELLS, wide))
                    for g in range(groups):
                        for half in range(halves):
                            weights.append(w_ref[half, g, 9 * i + 3 * j + k])
            term = jnp.dot(
                jnp.concatenate(windows, axis=1),
                jnp.concatenate(weights, axis=0),
                preferred_element_type=jnp.float32,
            )
            total = term if total is None else total + term
        total = jnp.maximum(total + bias, 0.0).reshape(4, 8, 2, 8, outs)
        for h in range(2):
            half = total[:, :, h].reshape(256, outs).T
            seg = slice(lb * CELLS + h * 256, lb * CELLS + (h + 1) * 256)
            o_ref[:, seg] = (half * act_ref[:, seg]).astype(jnp.bfloat16)


def convolve(spread, weight_all, active, share):
    halves, groups, _, part, outs = weight_all.shape
    vmem = pl.BlockSpec(memory_space=pltpu.VMEM)
    return pl.pallas_call(
        functools.partial(conv_kernel, share),
        in_specs=[vmem] * 3,
        out_specs=vmem,
        out_shape=jax.ShapeDtypeStruct((outs, share * CELLS), jnp.bfloat16),
        scratch_shapes=[
            pltpu.VMEM((share, ROWS, groups * halves * part), jnp.float32),
            pltpu.VMEM((3, share, 6, 10, 16, groups * halves * part), jnp.bfloat16),
        ],
        compiler_params=params(),
    )(spread, weight_all, active)


def return_kernel(groups, owners, v_ref, id_ref, p_ref, o_ref, found_ref, held, send_sem, recv_sem):
    width, low_cells = v_ref.shape[0] // groups, v_ref.shape[1]
    rows = id_ref.shape[2]
    me = greet("space", owners)
    spots = lax.broadcasted_iota(jnp.int32, (low_cells, rows), 0)

    def copy(t):
        return pltpu.make_async_remote_copy(
            src_ref=found_ref.at[t],
            dst_ref=held.at[t],
            send_sem=send_sem.at[t],
            recv_sem=recv_sem.at[t],
            device_id={"space": lax.rem(me + t, owners)},
            device_id_type=MESH,
        )

    def pick(s):
        ids = id_ref[s]
        high = ids // low_cells
        low = ids % low_cells
        onehot = jnp.where(spots == low, 1.0, 0.0).astype(jnp.bfloat16)
        found = jnp.dot(v_ref[...], onehot, preferred_element_type=jnp.float32)
        total = jnp.zeros((width, rows), jnp.float32)
        for g in range(groups):
            total = jnp.where(jnp.broadcast_to(high, total.shape) == g, found[g * width : (g + 1) * width], total)
        return total

    def add(d, values):
        at = pl.ds(pl.multiple_of(d * rows, rows), rows)
        o_ref[:, at] = (p_ref[:, at].astype(jnp.float32) + values).astype(jnp.bfloat16)

    def send(t, carry):
        found_ref[t] = pick(lax.rem(me + t, owners)).astype(jnp.bfloat16)
        copy(t).start()
        return carry

    def take(t, carry):
        copy(t).wait_recv()
        add(lax.rem(me + owners - t, owners), held[t].astype(jnp.float32))
        return carry

    def close(t, carry):
        copy(t).wait_send()
        return carry

    lax.fori_loop(1, owners, send, 0)
    add(me, pick(me))
    lax.fori_loop(1, owners, take, 0)
    lax.fori_loop(1, owners, close, 0)


def give_back(parts, ids, points, owners, cap):
    groups, width, low_cells = parts.shape
    vmem = pl.BlockSpec(memory_space=pltpu.VMEM)
    return pl.pallas_call(
        functools.partial(return_kernel, groups, owners),
        in_specs=[vmem] * 3,
        out_specs=vmem,
        out_shape=jax.ShapeDtypeStruct(points.shape, jnp.bfloat16),
        scratch_shapes=[
            pltpu.VMEM((owners, width, cap), jnp.bfloat16),
            pltpu.VMEM((owners, width, cap), jnp.bfloat16),
            pltpu.SemaphoreType.DMA((owners,)),
            pltpu.SemaphoreType.DMA((owners,)),
        ],
        compiler_params=remote_params(3),
    )(parts.reshape(groups * width, low_cells), ids.reshape(owners, 1, cap), points)


def tally_cells(ids, cells):
    fine = 64
    high = (ids[None, :] // fine == jnp.arange(cells // fine, dtype=jnp.int32)[:, None]).astype(jnp.bfloat16)
    low = (ids[None, :] % fine == jnp.arange(fine, dtype=jnp.int32)[:, None]).astype(jnp.bfloat16)
    return lax.dot_general(high, low, (((1,), (1,)), ((), ())), preferred_element_type=jnp.float32).reshape(cells)


def gather_half(conv_weight):
    half = conv_weight.shape[1] // 2
    mine = lax.dynamic_slice_in_dim(conv_weight, lax.rem(lax.axis_index("space"), 2) * half, half, 1)
    return lax.all_gather(mine, "chan", axis=0)


def swap_halves(gathered, owners):
    pairs = [[i, i + 1] for i in range(0, owners, 2)]
    return lax.all_gather(gathered, "space", axis=0, axis_index_groups=pairs)


def on_device(points, point_cell, conv_weight, conv_bias, neighbors):
    width = points.shape[0]
    owners = lax.axis_size("space")
    groups = lax.axis_size("chan")
    cap = points.shape[2] // owners
    blocks = neighbors.shape[0]
    share = blocks // groups
    flat = points.reshape(width, owners * cap)
    ids = point_cell[0]
    gathered = gather_half(conv_weight)
    counts = tally_cells(ids, blocks * CELLS)
    active = jnp.where(counts > 0.0, 1.0, 0.0).astype(jnp.float32)
    own = pool(flat, ids, counts, groups, owners, cap)
    left = lax.ppermute(own, "space", [(i, i + 1) for i in range(owners - 1)])
    right = lax.ppermute(own, "space", [(i + 1, i) for i in range(owners - 1)])
    margins = build_margins(neighbors, left, own, right, conv_bias.reshape(1, width), groups, share)
    gathered, margins = lax.optimization_barrier((gathered, margins))
    weight_all = swap_halves(gathered, owners)
    spread = exchange(margins, "chan", 1)
    mine = lax.dynamic_slice_in_dim(active, lax.axis_index("chan") * (share * CELLS), share * CELLS, 0)
    finished = convolve(spread, weight_all, mine.reshape(1, share * CELLS), share)
    finished = finished.reshape(groups, width, share * CELLS)
    parts = exchange(finished, "chan", 2)
    voxel_out = jnp.transpose(parts, (1, 0, 2)).reshape(width, blocks * CELLS)
    point_out = give_back(parts, ids, flat, owners, cap).reshape(points.shape)
    return (voxel_out, point_out)


def solution(mesh):
    return jax.shard_map(
        on_device,
        mesh=mesh,
        in_specs=(
            P("chan", "space", None),
            P("space", None),
            P(None, "chan", None),
            P("chan"),
            P("space", None),
        ),
        out_specs=(P("chan", "space"), P("chan", "space", None)),
        check_vma=False,
    )
```
